32 devices in a mesh: dp: 2 (over x), tensor: 4 (over y, core), expert: 4 (over z).
Axes of the slice: x: 2, y: 2, z: 4, core: 2. Of those that a mesh axis runs over, the one named last changes fastest.
Arguments:
- moe_input: bfloat16 [1024, 2048], P(('dp', 'tensor'), 'expert'), may hold values from -6 to 6
- grad_output: bfloat16 [1024, 2048], P(('dp', 'tensor'), 'expert'), may hold values from -6 to 6
- routes: int32 [1024, 8], P(('dp', 'tensor')), may hold values from 0 to 15, all different within a row; in each aligned block of 128 rows (0 to 127, 128 to 255, ...) at most 96 rows name the same one
- route_weight: float32 [1024, 8], P(('dp', 'tensor')), may hold values from 0.05 to 0.35
- capacity: int32 [16], replicated, may hold values from 48 to 96, as said below
- w_gate: bfloat16 [32, 384, 2048], P(('dp', 'tensor', 'expert')), may hold values from -0.125 to 0.125
- w_up: bfloat16 [32, 384, 2048], P(('dp', 'tensor', 'expert')), may hold values from -0.125 to 0.125
- w_down: bfloat16 [32, 384, 2048], P(('dp', 'tensor', 'expert')), may hold values from -0.21875 to 0.21875
Outputs:
- moe_output: bfloat16 [1024, 2048], P(('dp', 'tensor'), 'expert')
- grad_input: bfloat16 [1024, 2048], P(('dp', 'tensor'), 'expert')
- grad_gate: bfloat16 [32, 384, 2048], P(('dp', 'tensor', 'expert'))
- grad_up: bfloat16 [32, 384, 2048], P(('dp', 'tensor', 'expert'))
- grad_down: bfloat16 [32, 384, 2048], P(('dp', 'tensor', 'expert'))
The draws below stay inside these ranges and needn't reach their ends.
Inputs may be any that keep to these rules, and one draw needn't show every extreme that they name: `routes`: each row names 8 different experts; within each aligned block of 128 rows (the rows of one device) no expert is named more than 96 times. Some expert has a capacity of exactly 96.
All inputs are finite; a program needn't handle non-finite values.
Results may differ from the reference program's by a relative error of at most 0.0071.
Values may be sent and summed in bfloat16 or wider, within the bound.
No kernel may reach another device: no remote copies, remote signals or barrier semaphores. Data moves between devices by JAX's collectives and lax.ppermute only.
A program may use at most 128 MiB of HBM per device.

```python
import math
import jax
import jax.numpy as jnp
import numpy as np
from jax import lax

D = 2048
HID = 768
TOPK = 8
TOK_DEV = 128
EXPERTS = 16
MOST = 96
TOKENS = 1024
N_DP = 2
N_TENSOR = 4


def draw_capacity(key, part):
    inner = jax.random.fold_in(key, 17)
    key_caps, key_pick = jax.random.split(inner)
    base_caps = jax.random.randint(key_caps, (EXPERTS,), (MOST + 1) // 2, MOST + 1)
    chosen = jax.random.randint(key_pick, (), 0, EXPERTS)
    return jnp.where(jnp.arange(EXPERTS) == chosen, MOST, base_caps).astype(jnp.int32)


def level_of(own_key, dims, shards, low, largest):
    def one(position, parts):
        draws = jax.random.uniform(jax.random.fold_in(jax.random.fold_in(own_key, 6), position), (parts,), jnp.float32, low / len(shards), largest / len(shards))
        return jnp.repeat(jnp.exp(draws), dims[position] // parts).reshape((-1,) + (1,) * (len(dims) - position - 1))

    factor_of = one(*shards[0])
    for cut in shards[1:]:
        factor_of = factor_of * one(*cut)
    return factor_of


def assign_block(rng, own, number, rows, number_of, top, bound, lean):
    sequence = jax.random.permutation(rng, number_of)
    packed, ordinary = portions_of(number_of, rows * top, bound, lean, True), portions_of(number_of, rows * top, bound, lean, False)
    places = jnp.arange(number_of)

    def named(lengths, rotation):
        used = int((lengths > 0).sum())
        fixed = max(1, used // 4)
        shifted = fixed + (places - fixed + rotation * (used - fixed)) % max(1, number_of - fixed)
        return jnp.zeros((number_of,), jnp.int32).at[sequence[jnp.where(places < fixed, places, shifted)]].set(jnp.asarray(lengths, jnp.int32))

    lengths = jnp.where(number % 4 == 0, named(packed, number // 4), named(ordinary, number - number // 4 - 1))
    mixed = jax.random.permutation(jax.random.fold_in(own, 3), number_of)
    donor, receiver = mixed[0:number_of // 2 * 2:2], mixed[1:number_of // 2 * 2:2]
    room = jnp.minimum(lengths[donor] - 1, bound - lengths[receiver]) // 2
    room = jnp.where((donor == sequence[0]) | (receiver == sequence[0]) | (lengths[receiver] == 0), 0, jnp.maximum(room, 0))
    shifted = jax.random.randint(jax.random.fold_in(own, 4), (number_of // 2,), 0, 1 << 20) % (room + 1)
    lengths = lengths.at[donor].add(-shifted).at[receiver].add(shifted)
    members = jnp.searchsorted(jnp.cumsum(lengths), jnp.arange(rows * top), side="right").astype(jnp.int32)
    table = members.reshape(top, rows).T
    table = table[jax.random.permutation(jax.random.fold_in(own, 1), rows)]
    rotation = jax.random.randint(jax.random.fold_in(own, 2), (rows, 1), 0, top)
    return jnp.take_along_axis(table, (jnp.arange(top)[None, :] + rotation) % top, axis=1)


def portions_of(count, total, bound, lean, full):
    loads = [(1 << 20) // math.isqrt(rank ** lean) + 1 for rank in range(1, count + 1)]
    largest = bound if full else min(bound, max(-(-total // count), total * loads[0] // sum(loads)))
    least = 1 if total - largest >= count - 1 else 0
    holding, spare = [largest] + [least] * (count - 1), total - largest - least * (count - 1)
    while spare > 0:
        candidates = [i for i in range(1, count) if holding[i] < largest] or [i for i in range(1, count) if holding[i] < bound]
        whole, left = sum([loads[i] for i in candidates]), spare
        for i in candidates:
            extra = min(bound - holding[i], max(1, left * loads[i] // whole), spare)
            holding[i] = holding[i] + extra
            spare = spare - extra
    return np.array(holding)


def noise(own_key, extent, width, reach, shards=(), kind=jnp.bfloat16):
    values = jax.random.normal(own_key, extent, jnp.float32) * width
    if len(shards) > 0:
        values = level_of(own_key, extent, shards, -0.22, 0.18) * values
    return jnp.clip(values, min=-reach, max=reach).astype(kind)


def setup_inputs(seed: int = 0) -> dict:
    seeds = jax.random.split(jax.random.key(seed), 9)
    moe_input = noise(seeds[0], (TOKENS, D), 1.0, 6.0, ((0, 8), (1, 4)))
    grad_output = noise(seeds[1], (TOKENS, D), 1.0, 6.0, ((0, 8), (1, 4)))
    routes_keys = jax.random.split(jax.random.fold_in(seeds[2], 1), TOKENS // TOK_DEV)
    routes_turns = jax.random.permutation(jax.random.fold_in(seeds[2], 3), TOKENS // TOK_DEV)
    routes = jax.vmap(lambda own, number: assign_block(jax.random.fold_in(seeds[2], 2), own, number, TOK_DEV, EXPERTS, TOPK, MOST, 2))(routes_keys, routes_turns).reshape((TOKENS, TOPK))
    route_weight = jnp.clip(0.05 + 0.29999999 * jax.random.uniform(seeds[3], (TOKENS, TOPK), jnp.float32) ** level_of(seeds[3], (TOKENS, TOPK), ((0, 8),), -0.2, 0.2), 0.05, 0.35)
    capacity = draw_capacity(jax.random.fold_in(seeds[8], 71), 0)
    w_gate = noise(seeds[5], (2 * EXPERTS, HID // 2, D), D ** -0.5, 0.125, ((0, 32),))
    w_up = noise(seeds[6], (2 * EXPERTS, HID // 2, D), D ** -0.5, 0.125, ((0, 32),))
    w_down = noise(seeds[7], (2 * EXPERTS, HID // 2, D), HID ** -0.5, 0.21875, ((0, 32),))
    return {"moe_input": moe_input, "grad_output": grad_output, "routes": routes, "route_weight": route_weight, "capacity": capacity, "w_gate": w_gate, "w_up": w_up, "w_down": w_down}


def place_block(flat_routes, capacity):
    onehot = (flat_routes[:, None] == jnp.arange(EXPERTS, dtype=jnp.int32)[None, :]).astype(jnp.int32)
    before = jnp.cumsum(onehot, axis=0) - onehot
    pair_rank = jnp.sum(onehot * before, axis=1)
    pair_limit = jnp.sum(onehot * capacity[None, :], axis=1)
    pair_place = jnp.where(pair_rank < pair_limit, flat_routes * MOST + pair_rank, EXPERTS * MOST)
    return pair_place.astype(jnp.int32)


def spread_ints(pair_place, values):
    return jnp.full((EXPERTS * MOST + 1,), TOKENS, jnp.int32).at[pair_place].set(values)[:EXPERTS * MOST]


def spread_floats(pair_place, values):
    return jnp.zeros((EXPERTS * MOST + 1,), jnp.float32).at[pair_place].set(values)[:EXPERTS * MOST]


def reference(moe_input, grad_output, routes, route_weight, capacity, w_gate, w_up, w_down):
    groups = N_DP * N_TENSOR
    pair_count = TOK_DEV * TOPK
    half = HID // 2
    gate_all = w_gate.reshape(EXPERTS, HID, D)
    up_all = w_up.reshape(EXPERTS, HID, D)
    down_all = w_down.reshape(EXPERTS, HID, D)
    places = jax.vmap(place_block, in_axes=(0, None))(routes.reshape(groups, pair_count), capacity)
    pair_token = jnp.arange(pair_count, dtype=jnp.int32) // TOPK
    token_ids = pair_token[None, :] + (jnp.arange(groups, dtype=jnp.int32) * TOK_DEV)[:, None]
    slot_owner = jax.vmap(spread_ints)(places, token_ids)
    slot_weight = jax.vmap(spread_floats)(places, route_weight.reshape(groups, pair_count).astype(jnp.float32))
    owner_rows = slot_owner.reshape(groups, EXPERTS, MOST).transpose(1, 0, 2).reshape(EXPERTS, groups * MOST)
    weight_rows = slot_weight.reshape(groups, EXPERTS, MOST).transpose(1, 0, 2).reshape(EXPERTS, groups * MOST)
    padded_input = jnp.concatenate([moe_input, jnp.zeros((1, D), moe_input.dtype)], axis=0)
    padded_cot = jnp.concatenate([grad_output, jnp.zeros((1, D), grad_output.dtype)], axis=0)

    def expert_step(running, operands):
        slot_ids, weights, gate_w, up_w, down_w = operands
        slot_rows = padded_input[slot_ids]
        slot_cots = (weights[:, None] * padded_cot[slot_ids].astype(jnp.float32)).astype(jnp.bfloat16)
        gate_pre = jnp.dot(slot_rows, gate_w.T, preferred_element_type=jnp.float32)
        up_pre = jnp.dot(slot_rows, up_w.T, preferred_element_type=jnp.float32)
        sigmoid_gate = jax.nn.sigmoid(gate_pre)
        gate_act = gate_pre * sigmoid_gate
        hidden = (gate_act * up_pre).astype(jnp.bfloat16)
        hidden_cot = jnp.dot(slot_cots, down_w.T, preferred_element_type=jnp.float32)
        gate_cot = (hidden_cot * up_pre * sigmoid_gate * (1.0 + gate_pre * (1.0 - sigmoid_gate))).astype(jnp.bfloat16)
        up_cot = (hidden_cot * gate_act).astype(jnp.bfloat16)
        out_total = jnp.zeros((slot_rows.shape[0], D), jnp.float32)
        in_total = jnp.zeros((slot_rows.shape[0], D), jnp.float32)
        for part_index in range(2):
            low = part_index * half
            high = low + half
            out_part = lax.optimization_barrier(jnp.dot(hidden[:, low:high], down_w[low:high], preferred_element_type=jnp.float32).astype(jnp.bfloat16))
            in_sum = jnp.dot(gate_cot[:, low:high], gate_w[low:high], preferred_element_type=jnp.float32)
            in_sum = in_sum + jnp.dot(up_cot[:, low:high], up_w[low:high], preferred_element_type=jnp.float32)
            in_part = lax.optimization_barrier(in_sum.astype(jnp.bfloat16))
            out_total = out_total + out_part.astype(jnp.float32)
            in_total = in_total + in_part.astype(jnp.float32)
        expert_out = out_total.astype(jnp.bfloat16)
        input_slot = in_total.astype(jnp.bfloat16)
        out_acc, in_acc = running
        out_acc = out_acc.at[slot_ids].add(weights[:, None] * expert_out.astype(jnp.float32))
        in_acc = in_acc.at[slot_ids].add(input_slot.astype(jnp.float32))
        grad_gate = jnp.dot(gate_cot.T, slot_rows, preferred_element_type=jnp.float32).astype(jnp.bfloat16)
        grad_up = jnp.dot(up_cot.T, slot_rows, preferred_element_type=jnp.float32).astype(jnp.bfloat16)
        grad_down = jnp.dot(hidden.T, slot_cots, preferred_element_type=jnp.float32).astype(jnp.bfloat16)
        return (out_acc, in_acc), (grad_gate, grad_up, grad_down)

    start = (jnp.zeros((TOKENS + 1, D), jnp.float32), jnp.zeros((TOKENS + 1, D), jnp.float32))
    finals, grads = lax.scan(expert_step, start, (owner_rows, weight_rows, gate_all, up_all, down_all))
    out_acc, in_acc = finals
    grad_gate = grads[0].reshape(2 * EXPERTS, half, D)
    grad_up = grads[1].reshape(2 * EXPERTS, half, D)
    grad_down = grads[2].reshape(2 * EXPERTS, half, D)
    return out_acc[:TOKENS].astype(jnp.bfloat16), in_acc[:TOKENS].astype(jnp.bfloat16), grad_gate, grad_up, grad_down
```

```python
import functools

import jax
import jax.numpy as jnp
from jax import lax
from jax.experimental import pallas as pl
from jax.experimental.pallas import tpu as pltpu
from jax.sharding import PartitionSpec as P


NT = (((1,), (1,)), ((), ()))
NN = (((1,), (0,)), ((), ()))


def mm(a, b, dims):
    return lax.dot_general(a, b, dims, preferred_element_type=jnp.float32)


def route_body(routes_ref, weight_ref, cap_ref, out_ref):
    rows, topk = routes_ref.shape
    experts = out_ref.shape[1]
    lane = lax.broadcasted_iota(jnp.int32, (rows, experts), 1)
    named = jnp.zeros((rows, experts), jnp.float32)
    weight = jnp.zeros((rows, experts), jnp.float32)
    for k in range(topk):
        hit = routes_ref[:, k : k + 1] == lane
        named = named + jnp.where(hit, 1.0, 0.0)
        weight = weight + jnp.where(hit, weight_ref[:, k : k + 1], 0.0)
    row = lax.broadcasted_iota(jnp.int32, (rows, rows), 0)
    col = lax.broadcasted_iota(jnp.int32, (rows, rows), 1)
    earlier = jnp.where(col < row, 1.0, 0.0).astype(jnp.bfloat16)
    rank = mm(earlier, named.astype(jnp.bfloat16), NN)
    out_ref[...] = jnp.where(rank < cap_ref[...].astype(jnp.float32), weight, 0.0)


def route_weights(routes, route_weight, capacity):
    rows = routes.shape[0]
    experts = capacity.shape[0]
    return pl.pallas_call(
        route_body,
        out_shape=jax.ShapeDtypeStruct((rows, experts), jnp.float32),
        name="route",
    )(routes, route_weight, capacity.reshape(1, experts))


def forward_body(n, cols, place, *refs):
    blocks = refs[:n]
    w_ref, gate_ref, up_ref, down_ref = refs[n : n + 4]
    hid_ref, dg_ref, du_ref, mine_ref, peer_ref = refs[n + 4 : n + 9]
    g_acc, u_acc, hid = refs[n + 9 :]
    step = pl.program_id(0)

    @pl.when(step < cols)
    def _():
        x = jnp.concatenate([b[0] for b in blocks], axis=0)
        g = mm(x, gate_ref[0], NT)
        u = mm(x, up_ref[0], NT)

        @pl.when(step == 0)
        def _():
            g_acc[...] = g
            u_acc[...] = u

        @pl.when(step > 0)
        def _():
            g_acc[...] += g
            u_acc[...] += u

    @pl.when(step == cols)
    def _():
        lane = lax.broadcasted_iota(jnp.int32, w_ref.shape, 1)
        w = jnp.sum(jnp.where(lane == place[1], w_ref[...], 0.0), axis=1, keepdims=True)
        g = g_acc[...]
        u = u_acc[...]
        s = jax.nn.sigmoid(g)
        act = g * s
        wu = w * u
        hid[...] = (act * wu).astype(jnp.bfloat16)
        hid_ref[...] = hid[...]
        dg_ref[...] = wu * s * (1.0 + g * (1.0 - s))
        du_ref[...] = w * act

    @pl.when(step >= cols)
    def _():
        rows = blocks[0].shape[1]
        out = mm(hid[...], down_ref[0], NN).astype(jnp.bfloat16)
        for i in range(n // 2):
            mine_ref[i, 0] = out[2 * i * rows : (2 * i + 1) * rows]
            peer_ref[i, 0] = out[(2 * i + 1) * rows : (2 * i + 2) * rows]


def forward(place, blocks, weights, w_gate, w_up, w_down):
    n = len(blocks)
    cols, rows, width = blocks[0].shape
    hidden = w_gate.shape[1]
    total = n * rows
    first = lambda i: jnp.minimum(i, cols - 1)
    second = lambda i: jnp.maximum(i - cols, 0)
    block = pl.BlockSpec((1, rows, width), lambda i, s: (first(i), 0, 0))
    wide = pl.BlockSpec((1, hidden, width), lambda i, s: (0, 0, s[0] ^ first(i)))
    late = pl.BlockSpec((1, hidden, width), lambda i, s: (0, 0, s[0] ^ second(i)))
    whole = lambda a, b: pl.BlockSpec((a, b), lambda i, s: (0, 0))
    part = pl.BlockSpec((n // 2, 1, rows, width), lambda i, s: (0, second(i), 0, 0))
    half = jax.ShapeDtypeStruct((n // 2, cols, rows, width), jnp.bfloat16)
    return pl.pallas_call(
        functools.partial(forward_body, n, cols),
        grid_spec=pltpu.PrefetchScalarGridSpec(
            num_scalar_prefetch=1,
            grid=(2 * cols,),
            in_specs=[block] * n + [whole(*weights.shape), wide, wide, late],
            out_specs=[whole(total, hidden)] * 3 + [part] * 2,
            scratch_shapes=[
                pltpu.VMEM((total, hidden), jnp.float32),
                pltpu.VMEM((total, hidden), jnp.float32),
                pltpu.VMEM((total, hidden), jnp.bfloat16),
            ],
        ),
        out_shape=[
            jax.ShapeDtypeStruct((total, hidden), jnp.bfloat16),
            jax.ShapeDtypeStruct((total, hidden), jnp.float32),
            jax.ShapeDtypeStruct((total, hidden), jnp.float32),
            half,
            half,
        ],
        cost_estimate=pl.CostEstimate(
            flops=6 * total * hidden * width * cols,
            bytes_accessed=2 * (3 * hidden + 2 * total) * width * cols + 10 * total * hidden,
            transcendentals=total * hidden,
        ),
        name="forward",
    )(place, *blocks, weights, w_gate, w_up, w_down)


def backward_body(n, cols, place, *refs):
    blocks = refs[:n]
    dg_ref, du_ref, gate_ref, up_ref, down_ref = refs[n : n + 5]
    gc_ref, uc_ref, mine_ref, peer_ref = refs[n + 5 : n + 9]
    h_acc, gc, uc = refs[n + 9 :]
    step = pl.program_id(0)

    @pl.when(step < cols)
    def _():
        x = jnp.concatenate([b[0] for b in blocks], axis=0)
        h = mm(x, down_ref[0], NT)

        @pl.when(step == 0)
        def _():
            h_acc[...] = h

        @pl.when(step > 0)
        def _():
            h_acc[...] += h

    @pl.when(step == cols)
    def _():
        h = h_acc[...]
        gc[...] = (h * dg_ref[...]).astype(jnp.bfloat16)
        uc[...] = (h * du_ref[...]).astype(jnp.bfloat16)
        gc_ref[...] = gc[...]
        uc_ref[...] = uc[...]

    @pl.when(step >= cols)
    def _():
        rows = blocks[0].shape[1]
        out = mm(gc[...], gate_ref[0], NN) + mm(uc[...], up_ref[0], NN)
        out = out.astype(jnp.bfloat16)
        for i in range(n // 2):
            mine_ref[i, 0] = out[2 * i * rows : (2 * i + 1) * rows]
            peer_ref[i, 0] = out[(2 * i + 1) * rows : (2 * i + 2) * rows]


def backward(place, blocks, dg, du, w_gate, w_up, w_down):
    n = len(blocks)
    cols, rows, width = blocks[0].shape
    hidden = w_gate.shape[1]
    total = n * rows
    first = lambda i: jnp.minimum(i, cols - 1)
    second = lambda i: jnp.maximum(i - cols, 0)
    block = pl.BlockSpec((1, rows, width), lambda i, s: (first(i), 0, 0))
    wide = pl.BlockSpec((1, hidden, width), lambda i, s: (0, 0, s[0] ^ first(i)))
    late = pl.BlockSpec((1, hidden, width), lambda i, s: (0, 0, s[0] ^ second(i)))
    whole = lambda a, b: pl.BlockSpec((a, b), lambda i, s: (0, 0))
    part = pl.BlockSpec((n // 2, 1, rows, width), lambda i, s: (0, second(i), 0, 0))
    half = jax.ShapeDtypeStruct((n // 2, cols, rows, width), jnp.bfloat16)
    return pl.pallas_call(
        functools.partial(backward_body, n, cols),
        grid_spec=pltpu.PrefetchScalarGridSpec(
            num_scalar_prefetch=1,
            grid=(2 * cols,),
            in_specs=[block] * n + [whole(total, hidden)] * 2 + [late, late, wide],
            out_specs=[whole(total, hidden)] * 2 + [part] * 2,
            scratch_shapes=[
                pltpu.VMEM((total, hidden), jnp.float32),
                pltpu.VMEM((total, hidden), jnp.bfloat16),
                pltpu.VMEM((total, hidden), jnp.bfloat16),
            ],
        ),
        out_shape=[jax.ShapeDtypeStruct((total, hidden), jnp.bfloat16)] * 2 + [half] * 2,
        cost_estimate=pl.CostEstimate(
            flops=6 * total * hidden * width * cols,
            bytes_accessed=2 * (3 * hidden + 2 * total) * width * cols + 12 * total * hidden,
            transcendentals=0,
        ),
        name="backward",
    )(place, *blocks, dg, du, w_gate, w_up, w_down)


def grads_body(n, groups, place, *refs):
    xs = refs[:n]
    cs = refs[n : 2 * n]
    acts = refs[2 * n : 2 * n + 3 * groups]
    outs = refs[2 * n + 3 * groups : 2 * n + 3 * groups + 3]
    turned = refs[2 * n + 3 * groups + 3 :]

    @pl.when(pl.program_id(0) == 0)
    def _():
        for i in range(3):
            a = jnp.concatenate([r[...] for r in acts[i * groups : (i + 1) * groups]], axis=0)
            turned[i][...] = a.T

    x = jnp.concatenate([r[0] for r in xs], axis=0)
    outs[0][0] = mm(turned[0][...], x, NN).astype(jnp.bfloat16)
    outs[1][0] = mm(turned[1][...], x, NN).astype(jnp.bfloat16)
    c = jnp.concatenate([r[0] for r in cs], axis=0)
    outs[2][0] = mm(turned[2][...], c, NN).astype(jnp.bfloat16)


def grads(place, xs, cs, gcs, ucs, hids):
    n = len(xs)
    cols, rows, width = xs[0].shape
    hidden = gcs[0].shape[1]
    total = n * rows
    block = pl.BlockSpec((1, rows, width), lambda i, s: (i, 0, 0))
    acts = [*gcs, *ucs, *hids]
    out = pl.BlockSpec((1, hidden, width), lambda i, s: (0, 0, s[0] ^ i))
    return pl.pallas_call(
        functools.partial(grads_body, n, len(gcs)),
        grid_spec=pltpu.PrefetchScalarGridSpec(
            num_scalar_prefetch=1,
            grid=(cols,),
            in_specs=[block] * (2 * n)
            + [pl.BlockSpec(a.shape, lambda i, s: (0, 0)) for a in acts],
            out_specs=[out] * 3,
            scratch_shapes=[pltpu.VMEM((hidden, total), jnp.bfloat16)] * 3,
        ),
        out_shape=[jax.ShapeDtypeStruct((1, hidden, width * cols), jnp.bfloat16)] * 3,
        cost_estimate=pl.CostEstimate(
            flops=6 * total * hidden * width * cols,
            bytes_accessed=2 * (3 * hidden + 2 * total) * width * cols + 6 * total * hidden,
            transcendentals=0,
        ),
        name="grads",
    )(place, *xs, *cs, *acts)


def added(*terms):
    return sum(t.astype(jnp.float32) for t in terms).astype(jnp.bfloat16)


def dense_shards(moe_input, grad_output, routes, route_weight, capacity, w_gate, w_up, w_down):
    cols = lax.axis_size("expert")
    position = lax.axis_index("expert")
    per_group = capacity.shape[0] // lax.axis_size(("dp", "tensor"))
    group = lax.axis_index(("dp", "tensor"))
    expert = group * per_group + position * per_group // cols
    place = jnp.stack([position, expert]).astype(jnp.int32)

    def over(axis, flip):
        pairs = [(i, i ^ flip) for i in range(lax.axis_size(axis))]
        return lambda a: lax.ppermute(a, axis, pairs)

    core, over_y, over_x = over("tensor", 1), over("tensor", 2), over("dp", 1)

    def columns(a):
        return jnp.stack([a] + [over("expert", j)(a) for j in range(1, cols)])

    half = cols // 2
    x0 = columns(moe_input)
    weights = route_weights(routes, route_weight, capacity)
    for move in (core, over_y, over_x):
        weights = jnp.concatenate([weights, move(weights)], axis=0)
    rows = routes.shape[0]
    w = [weights[i * rows : (i + 1) * rows] for i in range(weights.shape[0] // rows)]
    c0 = columns(grad_output)
    x1, x2 = over_x(x0), over_y(x0)
    x3 = jnp.concatenate([over_x(x2[:half]), over_y(x1[half:])], axis=0)
    c1, c2 = over_x(c0), over_y(c0)
    c3 = jnp.concatenate([over_x(c2[:half]), over_y(c1[half:])], axis=0)
    xp = [core(a) for a in (x0, x1, x2, x3)]
    cp = [core(a) for a in (c0, c1, c2, c3)]
    ws = (w_gate, w_up, w_down)
    w_of = lambda *ids: jnp.concatenate([w[i] for i in ids], axis=0)
    hid0, dg0, du0, o0, p0 = forward(place, [x0, xp[0]], w_of(0, 1), *ws)
    hid1, dg1, du1, o1, p1 = forward(place, [x1, xp[1], x2, xp[2]], w_of(4, 5, 2, 3), *ws)
    hid3, dg3, du3, o3, p3 = forward(place, [x3, xp[3]], w_of(6, 7), *ws)
    gc0, uc0, i0, q0 = backward(place, [c0, cp[0]], dg0, du0, *ws)
    gc1, uc1, i1, q1 = backward(place, [c1, cp[1], c2, cp[2]], dg1, du1, *ws)
    gc3, uc3, i3, q3 = backward(place, [c3, cp[3]], dg3, du3, *ws)

    def home(m0, p0, m1, p1, m3, p3):
        r3 = added(m3[0], core(p3)[0])
        fx, fy = over_x(r3[:half]), over_y(r3[half:])
        r1p = core(p1)
        sx = jnp.concatenate([added(m1[0, :half], r1p[0, :half]), added(m1[0, half:], r1p[0, half:], fy)])
        sy = jnp.concatenate([added(m1[1, :half], r1p[1, :half], fx), added(m1[1, half:], r1p[1, half:])])
        r0 = added(m0[0], core(p0)[0], over_x(sx), over_y(sy))
        return added(r0[0], *[over("expert", j)(r0[j]) for j in range(1, cols)])

    moe_output = home(o0, p0, o1, p1, o3, p3)
    grad_input = home(i0, q0, i1, q1, i3, q3)
    xs = [x0, xp[0], x1, xp[1], x2, xp[2], x3, xp[3]]
    cs = [c0, cp[0], c1, cp[1], c2, cp[2], c3, cp[3]]
    grad_gate, grad_up, grad_down = grads(
        place, xs, cs, [gc0, gc1, gc3], [uc0, uc1, uc3], [hid0, hid1, hid3]
    )
    return (moe_output, grad_input, grad_gate, grad_up, grad_down)


def swapped(x, axis, apart):
    return lax.ppermute(x, axis, [(i, i ^ 1 << apart) for i in range(lax.axis_size(axis))])


def expert_work(slot_rows, slot_cots, gate_w, up_w, down_w):
    gate_pre = jnp.einsum("smd,hd->smh", slot_rows, gate_w, preferred_element_type=jnp.float32)
    up_pre = jnp.einsum("smd,hd->smh", slot_rows, up_w, preferred_element_type=jnp.float32)
    sigmoid_gate = jax.nn.sigmoid(gate_pre)
    gate_act = gate_pre * sigmoid_gate
    hidden = (gate_act * up_pre).astype(jnp.bfloat16)
    out_part = jnp.einsum("smh,hd->smd", hidden, down_w, preferred_element_type=jnp.float32).astype(
        jnp.bfloat16
    )
    hidden_cot = jnp.einsum("smd,hd->smh", slot_cots, down_w, preferred_element_type=jnp.float32)
    gate_cot = (
        hidden_cot * up_pre * sigmoid_gate * (1.0 + gate_pre * (1.0 - sigmoid_gate))
    ).astype(jnp.bfloat16)
    up_cot = (hidden_cot * gate_act).astype(jnp.bfloat16)
    in_sum = jnp.einsum("smh,hd->smd", gate_cot, gate_w, preferred_element_type=jnp.float32)
    in_sum = in_sum + jnp.einsum("smh,hd->smd", up_cot, up_w, preferred_element_type=jnp.float32)
    in_part = in_sum.astype(jnp.bfloat16)
    grad_gate = jnp.einsum(
        "smh,smd->hd", gate_cot, slot_rows, preferred_element_type=jnp.float32
    ).astype(jnp.bfloat16)
    grad_up = jnp.einsum(
        "smh,smd->hd", up_cot, slot_rows, preferred_element_type=jnp.float32
    ).astype(jnp.bfloat16)
    grad_down = jnp.einsum(
        "smh,smd->hd", hidden, slot_cots, preferred_element_type=jnp.float32
    ).astype(jnp.bfloat16)
    return (out_part, in_part, grad_gate[None], grad_up[None], grad_down[None])


def fill_slots(inputs, cots, owners, weights):
    filled = owners >= 0
    source = jnp.maximum(owners, 0)
    slot_rows = jnp.where(filled[..., None], inputs[source], jnp.zeros((), inputs.dtype))
    slot_cots = jnp.where(
        filled[..., None], weights[..., None] * cots[source].astype(jnp.float32), 0.0
    )
    return (slot_rows, slot_cots.astype(jnp.bfloat16))


def shards(moe_input, grad_output, routes, route_weight, capacity, w_gate, w_up, w_down):
    groups = lax.axis_size(("dp", "tensor"))
    position = lax.axis_index("expert")
    parity = position // 2
    half_index = position % 2
    tok_rows = routes.shape[0]
    topk = routes.shape[1]
    experts = capacity.shape[0]
    slot_depth = 12 * tok_rows // experts
    slot_count = experts * slot_depth
    pair_count = tok_rows * topk
    col_quarter = moe_input.shape[1]
    full_width = col_quarter * lax.axis_size("expert")
    half_width = full_width // 2
    flat_routes = routes.reshape(pair_count)
    onehot = (flat_routes[:, None] == jnp.arange(experts, dtype=jnp.int32)[None, :]).astype(
        jnp.int32
    )
    before = jnp.cumsum(onehot, axis=0) - onehot
    pair_rank = jnp.sum(onehot * before, axis=1)
    pair_limit = jnp.sum(onehot * capacity[None, :], axis=1)
    pair_kept = pair_rank < pair_limit
    pair_place = jnp.where(pair_kept, flat_routes * slot_depth + pair_rank, slot_count)
    pair_token = jnp.arange(pair_count, dtype=jnp.int32) // topk
    flat_weight = route_weight.reshape(pair_count)
    slot_owner = jnp.full((slot_count,), -1, jnp.int32).at[pair_place].set(pair_token, mode="drop")
    slot_weight = jnp.zeros((slot_count,), jnp.float32).at[pair_place].set(flat_weight, mode="drop")
    whole_input, whole_cot = (
        lax.all_gather(moe_input, "expert", axis=1, tiled=True),
        lax.all_gather(grad_output, "expert", axis=1, tiled=True),
    )
    owners = lax.dynamic_index_in_dim(
        slot_owner.reshape(groups, 2, slot_depth), parity, 1, keepdims=False
    )
    weights = lax.dynamic_index_in_dim(
        slot_weight.reshape(groups, 2, slot_depth), parity, 1, keepdims=False
    )
    send_rows, send_cots = fill_slots(whole_input, whole_cot, owners, weights)
    got_rows, got_cots = (
        lax.all_to_all(send_rows, ("dp", "tensor"), split_axis=0, concat_axis=0, tiled=True),
        lax.all_to_all(send_cots, ("dp", "tensor"), split_axis=0, concat_axis=0, tiled=True),
    )
    out_part, in_part, grad_gate, grad_up, grad_down = expert_work(
        got_rows, got_cots, w_gate[0], w_up[0], w_down[0]
    )
    out_split = out_part.reshape(groups, slot_depth, 2, half_width)
    in_split = in_part.reshape(groups, slot_depth, 2, half_width)
    mine_out = lax.dynamic_index_in_dim(out_split, half_index, 2, keepdims=False)
    mine_in = lax.dynamic_index_in_dim(in_split, half_index, 2, keepdims=False)
    other_out = lax.dynamic_index_in_dim(out_split, 1 - half_index, 2, keepdims=False)
    other_in = lax.dynamic_index_in_dim(in_split, 1 - half_index, 2, keepdims=False)
    peer_out, peer_in = swapped((other_out, other_in), "expert", 0)
    expert_out = (mine_out.astype(jnp.float32) + peer_out.astype(jnp.float32)).astype(jnp.bfloat16)
    input_slot = (mine_in.astype(jnp.float32) + peer_in.astype(jnp.float32)).astype(jnp.bfloat16)
    back_out, back_in = (
        lax.all_to_all(expert_out, ("dp", "tensor"), split_axis=0, concat_axis=0, tiled=True),
        lax.all_to_all(input_slot, ("dp", "tensor"), split_axis=0, concat_axis=0, tiled=True),
    )
    flat_out = back_out.reshape(groups * slot_depth, half_width)
    flat_in = back_in.reshape(groups * slot_depth, half_width)
    matched = pair_kept & (flat_routes % 2 == parity)
    back_place = jnp.where(matched, flat_routes // 2 * slot_depth + pair_rank, 0)
    pair_scale = jnp.where(matched, flat_weight, 0.0)
    pair_mask = jnp.where(matched, 1.0, 0.0)
    partial_out = jnp.sum(
        (flat_out[back_place].astype(jnp.float32) * pair_scale[:, None]).reshape(
            tok_rows, topk, half_width
        ),
        axis=1,
    )
    partial_in = jnp.sum(
        (flat_in[back_place].astype(jnp.float32) * pair_mask[:, None]).reshape(
            tok_rows, topk, half_width
        ),
        axis=1,
    )
    which_half = (jnp.arange(2, dtype=jnp.int32) == half_index)[None, :, None]
    placed_out = jnp.where(which_half, partial_out[:, None, :], 0.0).reshape(tok_rows, full_width)
    placed_in = jnp.where(which_half, partial_in[:, None, :], 0.0).reshape(tok_rows, full_width)
    moe_output, grad_input = (
        lax.psum_scatter(placed_out, "expert", scatter_dimension=1, tiled=True),
        lax.psum_scatter(placed_in, "expert", scatter_dimension=1, tiled=True),
    )
    return (
        moe_output.astype(jnp.bfloat16),
        grad_input.astype(jnp.bfloat16),
        grad_gate,
        grad_up,
        grad_down,
    )


def solution(mesh):
    in_specs = (
        P(("dp", "tensor"), "expert"),
        P(("dp", "tensor"), "expert"),
        P(("dp", "tensor"), None),
        P(("dp", "tensor"), None),
        P(),
        P(("dp", "tensor", "expert"), None, None),
        P(("dp", "tensor", "expert"), None, None),
        P(("dp", "tensor", "expert"), None, None),
    )
    out_specs = (
        P(("dp", "tensor"), "expert"),
        P(("dp", "tensor"), "expert"),
        P(("dp", "tensor", "expert"), None, None),
        P(("dp", "tensor", "expert"), None, None),
        P(("dp", "tensor", "expert"), None, None),
    )

    def dispatch(moe_input, grad_output, routes, *rest):
        tokens = moe_input.shape[0]
        shape = mesh.shape
        groups = shape["dp"] * shape["tensor"]
        expert_rows = 12 * tokens // rest[1].shape[0]
        paired = shape["dp"] == 2 and groups == 8 and shape["expert"] == 4
        plan = dense_shards if paired and 2 * expert_rows > tokens else shards
        call = jax.shard_map(plan, mesh=mesh, in_specs=in_specs, out_specs=out_specs, check_vma=False)
        return call(moe_input, grad_output, routes, *rest)

    return dispatch
```
